32 devices in a mesh: win: 2 (over y), px: 16 (over z, x, core).
Axes of the slice: x: 2, y: 2, z: 4, core: 2. Of those that a mesh axis runs over, the one named last changes fastest.
Arguments:
- charge_a: float32 [131072], P(('win', 'px')), parts along dimension 0, may hold values from -3 to 3
- charge_b: float32 [131072], P(('win', 'px')), parts along dimension 0, may hold values from -3 to 3
- coupling: float32 [2], P('win'), parts along dimension 0, may hold values from 0.1 to 0.9
- positions: float32 [3, 131072], P(None, ('win', 'px')), parts along dimension 1, may hold values from 0 to 128, as said below
- grid_base: int32 [3, 131072], P(None, ('win', 'px')), parts along dimension 1, may hold values from 0 to 127, as said below
- spline: float32 [3, 4, 131072], P(None, None, ('win', 'px')), parts along dimension 2, may hold values from 0 to 0.67, as said below
- spline_slope: float32 [3, 4, 131072], P(None, None, ('win', 'px')), parts along dimension 2, may hold values from -0.67 to 0.67, as said below
- influence: float32 [128, 128, 128], P(None, 'px'), may hold values from 0.5 to 300, as said below
- pair_tiles: int32 [1024, 12], P(('win', 'px')), parts along dimension 0, may hold values from 0 to 39
- ghost_lists: int32 [2, 16384], P(None, ('win', 'px')), parts along dimension 1, may hold values from 0 to 4095
Outputs:
- forces: float32 [3, 131072], P(None, ('win', 'px')), parts along dimension 1
The draws below stay inside these ranges and needn't reach their ends.
There are 2 independent parts, one for each index of `win`. The reference program is written for one: setup_inputs(seed, part) draws one part's arguments, and reference() takes and returns one part's arrays. A program takes and returns all parts, laid end to end along the dimension named above; an argument that names none is the same for every part. Nothing has to cross between parts.
Inputs may be any that keep to these rules, and one draw needn't show every extreme that they name: `grid_base`: row 0 of atom i lies in [d * 8, (d + 1) * 8) for d = i // 4096; rows 1 and 2 lie in [0, 128). `positions`: row 0 of atom i lies in [d * 8, (d + 1) * 8) for d = i // 4096; rows 1 and 2 lie in [0, 8). For each atom and dimension, the 4 cubic B-spline weights at some fraction u in [0, 1). `spline_slope`: the derivatives in u of the weights in spline, at the same u. influence at wave index m equals influence at -m, indices taken modulo the grid's lengths.
All inputs are finite; a program needn't handle non-finite values.
Results may differ from the reference program's by a relative error of at most 0.0003.
Values sent between devices are 32-bit elements; how exact they have to be, the bound alone decides.
A program may use at most 256 MiB of HBM per device.

```python
import math
import jax
import jax.numpy as jnp
from jax import lax

KX = 128
KY = 128
KZ = 128
ORDER = 4
TILE = 128
NBR = 12
ATOMS_DEV = 4096
GH_DEV = 512
PLANES = 8
ATOMS = 65536
GHOSTS = 8192
N_PX = 16


def draw_grid_base(key, part):
    key_x, key_y, key_z = jax.random.split(jax.random.fold_in(key, 11), 3)
    atom_ids = jnp.arange(ATOMS, dtype=jnp.int32)
    slab_start = atom_ids // ATOMS_DEV * PLANES
    row_x = slab_start + jax.random.randint(key_x, (ATOMS,), 0, PLANES, dtype=jnp.int32)
    row_y = jax.random.randint(key_y, (ATOMS,), 0, KY, dtype=jnp.int32)
    row_z = jax.random.randint(key_z, (ATOMS,), 0, KZ, dtype=jnp.int32)
    return jnp.stack([row_x, row_y, row_z]).astype(jnp.int32)


def spline_fraction(key):
    return jax.random.uniform(jax.random.fold_in(key, 23), (3, ATOMS), jnp.float32)


def draw_spline(key, part):
    fraction = spline_fraction(key)
    remain = 1.0 - fraction
    cube = fraction * fraction * fraction
    square = fraction * fraction
    weights = [remain * remain * remain / 6.0, (3.0 * cube - 6.0 * square + 4.0) / 6.0, (-3.0 * cube + 3.0 * square + 3.0 * fraction + 1.0) / 6.0, cube / 6.0]
    return jnp.stack(weights, axis=1).astype(jnp.float32)


def draw_spline_slope(key, part):
    fraction = spline_fraction(key)
    remain = 1.0 - fraction
    square = fraction * fraction
    slopes = [-remain * remain / 2.0, (3.0 * square - 4.0 * fraction) / 2.0, (-3.0 * square + 2.0 * fraction + 1.0) / 2.0, square / 2.0]
    return jnp.stack(slopes, axis=1).astype(jnp.float32)


def draw_positions(key, part):
    key_x, key_y = jax.random.split(jax.random.fold_in(key, 37), 2)
    atom_ids = jnp.arange(ATOMS, dtype=jnp.int32)
    slab_start = (atom_ids // ATOMS_DEV * PLANES).astype(jnp.float32)
    inside = jax.random.uniform(key_x, (ATOMS,), jnp.float32)
    across = 8.0 * jax.random.uniform(key_y, (2, ATOMS), jnp.float32)
    row_x = slab_start + PLANES * inside * 0.999
    return jnp.concatenate([row_x[None], across * 0.999], axis=0).astype(jnp.float32)


def draw_influence(key, part):
    lowest, highest = (1.0, 100.0)
    exponent = jax.random.uniform(jax.random.fold_in(key, 53), (KX, KY, KZ), jnp.float32, jnp.log(lowest), jnp.log(highest))
    base_field = jnp.exp(exponent)
    mirror = jnp.roll(jnp.flip(base_field, axis=(0, 1, 2)), 1, axis=(0, 1, 2))
    return (0.5 * (base_field + mirror)).astype(jnp.float32)


def plant(entries, key, low, high):
    spot = [jax.random.randint(jax.random.fold_in(key, axis), (), 0, length) for axis, length in enumerate(entries.shape)]
    longest = entries.shape.index(max(entries.shape))
    neighbour = spot[:longest] + [(spot[longest] + 1) % entries.shape[longest]] + spot[longest + 1:]
    return entries.at[tuple(spot)].set(low).at[tuple(neighbour)].set(high)


def level_of(rng, shape, cuts, low, largest):
    def one(axis_at, parts):
        steps = jax.random.uniform(jax.random.fold_in(jax.random.fold_in(rng, 6), axis_at), (parts,), jnp.float32, low / len(cuts), largest / len(cuts))
        return jnp.repeat(jnp.exp(steps), shape[axis_at] // parts).reshape((-1,) + (1,) * (len(shape) - axis_at - 1))

    gain = one(*cuts[0])
    for cut in cuts[1:]:
        gain = gain * one(*cut)
    return gain


def scatter_about(key, extent, spread, reach, shards=(), held_as=jnp.bfloat16):
    result = spread * jax.random.normal(key, extent, jnp.float32)
    if shards:
        result = result * level_of(key, extent, shards, -0.22, 0.18)
    return jnp.clip(result, -reach, reach).astype(held_as)


def setup_inputs(seed: int = 0, part: int = 0) -> dict:
    key_of = jax.random.split(jax.random.key(seed), 11)
    own_keys = jax.random.split(jax.random.fold_in(key_of[10], part), 11)
    charge_a = scatter_about(own_keys[0], (ATOMS,), 0.5, 3.0, ((0, 16),), jnp.float32)
    charge_b = scatter_about(own_keys[1], (ATOMS,), 0.5, 3.0, ((0, 16),), jnp.float32)
    coupling = jnp.clip(jax.random.uniform(own_keys[2], (1,), jnp.float32, 0.1, 0.9), 0.1, 0.9)
    positions = draw_positions(jax.random.fold_in(jax.random.fold_in(key_of[10], part), 71), part)
    grid_base = draw_grid_base(jax.random.fold_in(jax.random.fold_in(key_of[10], part), 71), part)
    spline = draw_spline(jax.random.fold_in(jax.random.fold_in(key_of[10], part), 71), part)
    spline_slope = draw_spline_slope(jax.random.fold_in(jax.random.fold_in(key_of[10], part), 71), part)
    influence = draw_influence(jax.random.fold_in(key_of[10], 71), part)
    pair_tiles = plant(jax.random.randint(own_keys[8], (ATOMS // TILE, NBR), 0, (ATOMS_DEV + 2 * GH_DEV) // TILE), jax.random.fold_in(own_keys[8], 1), 0, ((ATOMS_DEV + 2 * GH_DEV) // TILE) - 1).astype(jnp.int32)
    ghost_lists = plant(jax.random.randint(own_keys[9], (2, GHOSTS), 0, ATOMS_DEV), jax.random.fold_in(own_keys[9], 1), 0, ATOMS_DEV - 1).astype(jnp.int32)
    return dict(charge_a=charge_a, charge_b=charge_b, coupling=coupling, positions=positions, grid_base=grid_base, spline=spline, spline_slope=spline_slope, influence=influence, pair_tiles=pair_tiles, ghost_lists=ghost_lists)


ewald_beta = 0.35
soften_sq = 0.25

def pair_block(home_rows, nearby, weight_b):
    separation = home_rows[0:3, :, :, None] - nearby[0:3, :, None, :]
    dist_sq = lax.optimization_barrier(jnp.sum(separation * separation, axis=0)) + soften_sq
    distance = jnp.sqrt(dist_sq)
    radial = (jax.scipy.special.erfc(ewald_beta * distance) / distance + 2.0 * ewald_beta / math.sqrt(math.pi) * jnp.exp(-ewald_beta * ewald_beta * dist_sq)) / dist_sq
    mixed = (1.0 - weight_b) * home_rows[3][:, :, None] * nearby[3][:, None, :] + weight_b * home_rows[4][:, :, None] * nearby[4][:, None, :]
    return lax.optimization_barrier(jnp.sum((mixed * radial)[None] * separation, axis=3))

def device_pairs(home_rows, candidates, tile_list, weight_b):
    home_tiles = home_rows.reshape(5, -1, TILE)
    cand_tiles = candidates.reshape(5, -1, TILE)

    def one_slot(accumulated, column):
        nearby = jnp.take(cand_tiles, column, axis=1)
        return (accumulated + pair_block(home_tiles, nearby, weight_b), None)
    start = jnp.zeros((3,) + home_tiles.shape[1:], jnp.float32)
    accumulated, unused = lax.scan(one_slot, start, tile_list.T)
    return accumulated.reshape(3, -1)

def reference(charge_a, charge_b, coupling, positions, grid_base, spline, spline_slope, influence, pair_tiles, ghost_lists):
    weight_b = coupling[0]
    charges = jnp.stack([charge_a, charge_b])
    charge_grid = jnp.zeros((2, KX, KY, KZ), jnp.float32)
    for offset_x in range(ORDER):
        for offset_y in range(ORDER):
            for offset_z in range(ORDER):
                index_x = (grid_base[0] + offset_x) % KX
                index_y = (grid_base[1] + offset_y) % KY
                index_z = (grid_base[2] + offset_z) % KZ
                weight = spline[0, offset_x] * spline[1, offset_y] * spline[2, offset_z]
                charge_grid = charge_grid.at[:, index_x, index_y, index_z].add(charges * weight[None])
    spectrum = jnp.fft.fftn(charge_grid, axes=(1, 2, 3)) * influence[None]
    potential = jnp.real(jnp.fft.ifftn(spectrum, axes=(1, 2, 3))).astype(jnp.float32)
    gradient = jnp.zeros((3, 2, ATOMS), jnp.float32)
    for offset_x in range(ORDER):
        for offset_y in range(ORDER):
            for offset_z in range(ORDER):
                index_x = (grid_base[0] + offset_x) % KX
                index_y = (grid_base[1] + offset_y) % KY
                index_z = (grid_base[2] + offset_z) % KZ
                sample = potential[:, index_x, index_y, index_z]
                part_x = spline_slope[0, offset_x] * spline[1, offset_y] * spline[2, offset_z]
                part_y = spline[0, offset_x] * spline_slope[1, offset_y] * spline[2, offset_z]
                part_z = spline[0, offset_x] * spline[1, offset_y] * spline_slope[2, offset_z]
                gradient = gradient + jnp.stack([part_x, part_y, part_z])[:, None] * sample[None]
    reciprocal = -((1.0 - weight_b) * charge_a * gradient[:, 0] + weight_b * charge_b * gradient[:, 1])
    packet = jnp.concatenate([positions, charge_a[None], charge_b[None]], axis=0).reshape(5, N_PX, ATOMS_DEV)
    ghost_table = ghost_lists.reshape(2, N_PX, GH_DEV)
    to_right = jnp.take_along_axis(packet, jnp.broadcast_to(ghost_table[0][None], (5, N_PX, GH_DEV)), axis=2)
    to_left = jnp.take_along_axis(packet, jnp.broadcast_to(ghost_table[1][None], (5, N_PX, GH_DEV)), axis=2)
    from_left = jnp.roll(to_right, 1, axis=1)
    from_right = jnp.roll(to_left, -1, axis=1)
    device_ids = jnp.arange(N_PX, dtype=jnp.int32)
    from_left = from_left.at[0].add(-KX * (device_ids == 0).astype(jnp.float32)[:, None])
    from_right = from_right.at[0].add(KX * (device_ids == N_PX - 1).astype(jnp.float32)[:, None])
    candidates = jnp.concatenate([packet, from_left, from_right], axis=2)
    tile_lists = pair_tiles.reshape(N_PX, ATOMS_DEV // TILE, NBR)

    def one_device(inputs):
        return device_pairs(inputs[0], inputs[1], inputs[2], weight_b)
    real_space = lax.map(one_device, (jnp.moveaxis(packet, 1, 0), jnp.moveaxis(candidates, 1, 0), tile_lists))
    real_space = jnp.moveaxis(real_space, 0, 1).reshape(3, ATOMS)
    return reciprocal + real_space
```

```python
import functools
import math

import jax
import jax.numpy as jnp
from jax import lax
from jax.experimental import pallas as pl
from jax.experimental.pallas import tpu as pltpu
from jax.sharding import PartitionSpec as P

TILE = 128

high = lax.Precision.HIGH
ewald_beta = 0.35
soften_sq = 0.25
t_scale = 0.13
t_poly = (
    0.2093298660627116,
    0.2140488115708388,
    0.1607995042093057,
    0.2997555766949459,
    -0.16268460574346366,
    0.41880827459241754,
    -0.14005895059197282,
)


def from_behind(value, axis, steps):
    count = lax.axis_size(axis)
    pairs = [(source, (source + steps) % count) for source in range(count)]
    return lax.ppermute(value, axis, pairs)


def phase_tables(rows, length):
    wave_index = jnp.arange(length, dtype=jnp.int32)
    angle = (
        2.0 * math.pi / length * (rows[:, None] * wave_index[None, :] % length).astype(jnp.float32)
    )
    return jnp.cos(angle), jnp.sin(angle)


def forward_matrix(rows, length):
    c, s = phase_tables(rows, length)
    return jnp.stack([jnp.stack([c, -s], axis=1), jnp.stack([s, c], axis=1)])


def inverse_matrix(rows, length):
    c, s = phase_tables(rows, length)
    c, s = c.T, s.T
    return jnp.stack([jnp.stack([c, s], axis=1), jnp.stack([-s, c], axis=1)])


def split(value):
    upper = value.astype(jnp.bfloat16)
    lower = (value - upper.astype(jnp.float32)).astype(jnp.bfloat16)
    return upper, lower


def dot3(a_hi, a_lo, b_hi, b_lo):
    mm = functools.partial(jnp.dot, preferred_element_type=jnp.float32)
    return mm(a_hi, b_hi) + mm(a_lo, b_hi) + mm(a_hi, b_lo)


def banded(cells, base, weights, length):
    gap = cells - base
    if length is not None:
        gap = jnp.where(gap < 0.0, gap + float(length), gap)
    results = [jnp.zeros(gap.shape, jnp.float32) for unused in weights]
    for offset in range(len(weights[0])):
        here = gap == float(offset)
        results = [
            jnp.where(here, group[offset], value) for group, value in zip(weights, results)
        ]
    return results


def cells_of(shape, dim):
    return lax.broadcasted_iota(jnp.int32, shape, dim).astype(jnp.float32)


def spread_kernel(rows_ref, cols_ref, out_ref, hi_ref, lo_ref, *, order, width, full_y, full_z):
    count = rows_ref.shape[1]

    def row(k):
        return rows_ref[k : k + 1, :]

    def col(k):
        return cols_ref[:, k : k + 1]

    padded = -(-width // 8) * 8
    (band_x,) = banded(
        cells_of((padded, count), 0), row(0), [[row(3 + o) for o in range(order)]], None
    )
    (band_y,) = banded(
        cells_of((full_y, count), 0), row(1), [[row(3 + order + o) for o in range(order)]], full_y
    )
    for p in range(width):
        upper, lower = split(band_y * band_x[p : p + 1, :])
        hi_ref[p * full_y : (p + 1) * full_y, :] = upper
        lo_ref[p * full_y : (p + 1) * full_y, :] = lower
    (band_z,) = banded(
        cells_of((count, full_z), 1),
        col(2),
        [[col(3 + 2 * order + o) for o in range(order)]],
        full_z,
    )
    q = 3 + 6 * order
    z_hi, z_lo = split(jnp.concatenate([col(q) * band_z, col(q + 1) * band_z], axis=1))
    total = dot3(hi_ref[...], lo_ref[...], z_hi, z_lo)

    @pl.when(pl.program_id(0) == 0)
    def _():
        out_ref[...] = total

    @pl.when(pl.program_id(0) > 0)
    def _():
        out_ref[...] += total


def gather_kernel(
    cols_ref, grid_ref, pairs_ref, out_ref, hi_ref, lo_ref, *, order, width, full_y, full_z
):
    count = cols_ref.shape[0]

    @pl.when(pl.program_id(0) == 0)
    def _():
        upper, lower = split(grid_ref[...])
        hi_ref[...] = upper
        lo_ref[...] = lower

    def col(k):
        return cols_ref[:, k : k + 1]

    def groups(axis):
        return [
            [col(3 + axis * order + o) for o in range(order)],
            [col(3 + (3 + axis) * order + o) for o in range(order)],
        ]

    plain_x, slope_x = banded(cells_of((count, 128), 1), col(0), groups(0), None)
    plain_y, slope_y = banded(cells_of((count, full_y), 1), col(1), groups(1), full_y)
    plain_z, slope_z = banded(cells_of((count, full_z), 1), col(2), groups(2), full_z)
    q = 3 + 6 * order
    weight_a, weight_b = col(q + 2), col(q + 3)
    tables = hi_ref[...], lo_ref[...]
    plain = dot3(
        *split(jnp.concatenate([weight_a * plain_z, weight_b * plain_z], axis=1)), *tables
    )
    slope = dot3(
        *split(jnp.concatenate([weight_a * slope_z, weight_b * slope_z], axis=1)), *tables
    )
    sum_x = jnp.zeros((count, full_y), jnp.float32)
    sum_y = sum_x
    sum_z = sum_x
    for p in range(width):
        here = slice(p * full_y, (p + 1) * full_y)
        weight, lean = plain_x[:, p : p + 1], slope_x[:, p : p + 1]
        sum_x = sum_x + lean * plain[:, here]
        sum_y = sum_y + weight * plain[:, here]
        sum_z = sum_z + weight * slope[:, here]
    values = (sum_x * plain_y, sum_y * slope_y, sum_z * plain_y)
    for k, value in enumerate(values):
        out_ref[:, k : k + 1] = pairs_ref[:, k : k + 1] + jnp.sum(value, axis=1, keepdims=True)


def pair_kernel(tiles_ref, home_ref, cand_ref, out_ref, *, chunk):
    t = pl.program_id(0)
    slots = tiles_ref.shape[1]
    for start in range(0, TILE, chunk):
        here = slice(start, start + chunk)
        home = [
            jnp.broadcast_to(home_ref[here, k : k + 1], (chunk, TILE)) for k in range(5)
        ]
        total = [jnp.zeros((chunk, TILE), jnp.float32) for unused in range(3)]
        for slot in range(slots):
            k = tiles_ref[t, slot]
            near = cand_ref[k]
            gaps = [home[d] - near[d : d + 1, :] for d in range(3)]
            dist_sq = gaps[0] * gaps[0] + gaps[1] * gaps[1] + gaps[2] * gaps[2] + soften_sq
            inverse = lax.rsqrt(dist_sq)
            t_value = pl.reciprocal(1.0 + t_scale * (dist_sq * inverse))
            poly = t_poly[-1]
            for factor in t_poly[-2::-1]:
                poly = poly * t_value + factor
            bracket = poly * (t_value * inverse) + 2.0 * ewald_beta / math.sqrt(math.pi)
            decay = jnp.exp2(dist_sq * (-ewald_beta * ewald_beta * math.log2(math.e)))
            mixed = home[3] * near[3:4, :] + home[4] * near[4:5, :]
            weight = (mixed * decay) * (bracket * (inverse * inverse))
            total = [value + weight * gap for value, gap in zip(total, gaps)]
        for d in range(3):
            out_ref[here, d : d + 1] = jnp.sum(total[d], axis=1, keepdims=True)


def per_device(
    charge_a,
    charge_b,
    coupling,
    positions,
    grid_base,
    spline,
    spline_slope,
    influence,
    pair_tiles,
    ghost_lists,
):
    group_size = lax.axis_size("px")
    me_index = lax.axis_index("px")
    atom_count = charge_a.shape[0]
    full_x, slab_y, full_z = influence.shape
    full_y = slab_y * group_size
    planes = full_x // group_size
    order = spline.shape[1]
    width = planes + order - 1
    cells = width * full_y
    weight_b = coupling[0]
    scale = 1.0 / (full_x * full_y * full_z)

    packet = jnp.concatenate([positions, charge_a[None], charge_b[None]], axis=0)
    by_atom = packet.T
    from_left = from_behind(jnp.take(by_atom, ghost_lists[0], axis=0).T, "px", 1)
    from_right = from_behind(jnp.take(by_atom, ghost_lists[1], axis=0).T, "px", -1)

    base = jnp.stack([grid_base[0] - me_index * planes, grid_base[1], grid_base[2]])
    rows = jnp.concatenate(
        [
            base.astype(jnp.float32),
            spline.reshape(3 * order, atom_count),
            spline_slope.reshape(3 * order, atom_count),
            charge_a[None],
            charge_b[None],
            (-scale * (1.0 - weight_b) * charge_a)[None],
            (-scale * weight_b * charge_b)[None],
        ],
        axis=0,
    )
    rows = jnp.pad(rows, ((0, -rows.shape[0] % 8), (0, 0)))
    fields = rows.shape[0]
    cols = rows.T

    block = min(512, atom_count)
    sizes = dict(order=order, width=width, full_y=full_y, full_z=full_z)
    spread = pl.pallas_call(
        functools.partial(spread_kernel, **sizes),
        grid=(atom_count // block,),
        in_specs=[
            pl.BlockSpec((fields, block), lambda i: (0, i)),
            pl.BlockSpec((block, fields), lambda i: (i, 0)),
        ],
        out_specs=pl.BlockSpec((cells, 2 * full_z), lambda i: (0, 0)),
        out_shape=jax.ShapeDtypeStruct((cells, 2 * full_z), jnp.float32),
        scratch_shapes=[pltpu.VMEM((cells, block), jnp.bfloat16)] * 2,
        compiler_params=pltpu.CompilerParams(vmem_limit_bytes=56 << 20),
        cost_estimate=pl.CostEstimate(
            flops=12 * atom_count * cells * full_z, bytes_accessed=4 << 20, transcendentals=0
        ),
        name="spread",
    )(rows, cols)

    slab_rows = (
        jnp.arange(group_size, dtype=jnp.int32)[:, None] * planes
        + jnp.arange(width, dtype=jnp.int32)[None, :]
    ).reshape(-1) % full_x
    range_y = jnp.arange(full_y, dtype=jnp.int32)
    range_z = jnp.arange(full_z, dtype=jnp.int32)
    along_z = forward_matrix(range_z, full_z).reshape(2 * full_z, 2, full_z)
    waves = jnp.einsum("pyc,cdk->dpyk", spread.reshape(width, full_y, 2 * full_z), along_z, precision=high)
    waves = jnp.einsum("dpyk,dyew->epwk", waves, forward_matrix(range_y, full_y), precision=high)
    columns = lax.all_to_all(waves, "px", split_axis=2, concat_axis=1, tiled=True)
    columns = jnp.einsum("dxwk,dxeu->euwk", columns, forward_matrix(slab_rows, full_x), precision=high)
    columns = columns * influence[None]
    columns = jnp.einsum("duwk,duex->exwk", columns, inverse_matrix(slab_rows, full_x), precision=high)
    returned = lax.all_to_all(columns, "px", split_axis=1, concat_axis=2, tiled=True)
    returned = jnp.einsum("dpwk,dwey->ekpy", returned, inverse_matrix(range_y, full_y), precision=high)
    potential = jnp.einsum("dkpy,dkez->ezpy", returned, inverse_matrix(range_z, full_z), precision=high)
    potential = potential.reshape(2 * full_z, cells)

    shift = jnp.where(me_index == 0, -float(full_x), 0.0)
    from_left = jnp.concatenate([from_left[:1] + shift, from_left[1:]], axis=0)
    shift = jnp.where(me_index == group_size - 1, float(full_x), 0.0)
    from_right = jnp.concatenate([from_right[:1] + shift, from_right[1:]], axis=0)
    candidates = jnp.concatenate([packet, from_left, from_right], axis=1)
    cand_tiles = candidates.reshape(5, -1, TILE).transpose(1, 0, 2)
    cand_tiles = jnp.pad(cand_tiles, ((0, 0), (0, 3), (0, 0)))
    home = jnp.concatenate(
        [
            positions,
            ((1.0 - weight_b) * charge_a)[None],
            (weight_b * charge_b)[None],
            jnp.zeros((3, atom_count), jnp.float32),
        ],
        axis=0,
    ).T
    tile_count, slots = pair_tiles.shape
    pair_work = tile_count * slots * TILE * TILE
    pairs = pl.pallas_call(
        functools.partial(pair_kernel, chunk=32),
        grid_spec=pltpu.PrefetchScalarGridSpec(
            num_scalar_prefetch=1,
            grid=(tile_count,),
            in_specs=[
                pl.BlockSpec((TILE, 8), lambda i, tiles: (i, 0)),
                pl.BlockSpec(cand_tiles.shape, lambda i, tiles: (0, 0, 0)),
            ],
            out_specs=pl.BlockSpec((TILE, 8), lambda i, tiles: (i, 0)),
        ),
        out_shape=jax.ShapeDtypeStruct((atom_count, 8), jnp.float32),
        cost_estimate=pl.CostEstimate(
            flops=50 * pair_work, bytes_accessed=4 << 20, transcendentals=3 * pair_work
        ),
        name="pairs",
    )(pair_tiles, home, cand_tiles)

    block = min(256, atom_count)
    forces = pl.pallas_call(
        functools.partial(gather_kernel, **sizes),
        grid=(atom_count // block,),
        in_specs=[
            pl.BlockSpec((block, fields), lambda i: (i, 0)),
            pl.BlockSpec((2 * full_z, cells), lambda i: (0, 0)),
            pl.BlockSpec((block, 8), lambda i: (i, 0)),
        ],
        out_specs=pl.BlockSpec((block, 8), lambda i: (i, 0)),
        out_shape=jax.ShapeDtypeStruct((atom_count, 8), jnp.float32),
        scratch_shapes=[pltpu.VMEM((2 * full_z, cells), jnp.bfloat16)] * 2,
        compiler_params=pltpu.CompilerParams(vmem_limit_bytes=56 << 20),
        cost_estimate=pl.CostEstimate(
            flops=24 * atom_count * cells * full_z, bytes_accessed=6 << 20, transcendentals=0
        ),
        name="gather",
    )(cols, potential, pairs)
    return forces[:, :3].T


def solution(mesh):
    placed = (
        P(("win", "px")),
        P(("win", "px")),
        P("win"),
        P(None, ("win", "px")),
        P(None, ("win", "px")),
        P(None, None, ("win", "px")),
        P(None, None, ("win", "px")),
        P(None, "px", None),
        P(("win", "px"), None),
        P(None, ("win", "px")),
    )
    return jax.shard_map(
        per_device, mesh=mesh, in_specs=placed, out_specs=P(None, ("win", "px")), check_vma=False
    )
```
